512 devices in a mesh: dim: 16 (over z_hi, y, core), row: 32 (over x, z_lo).
Axes of the slice: x: 4, y: 4, z: 16 (z_hi: 2, z_lo: 8; z = z_hi * 8 + z_lo), core: 2. Of those that a mesh axis runs over, the one named last changes fastest.
Arguments:
- vectors: bfloat16 [53248, 4096], P('row', 'dim'), may hold values from -6 to 6
- blocks: float32 [5, 4096, 128], P(None, 'dim'), may hold values from -0.5 to 0.5
- angles: float32 [5, 4096], P(None, 'dim'), may hold values from -3.140625 to 3.140625
- codes: int32 [53248, 4096], P('row', 'dim'), may hold values from 0 to 15
- scale_index: int32 [53248], P('row'), may hold values from 0 to 15
- scale_table: float32 [16], replicated, may hold values from 0.05 to 0.3
- block_state: float32 [5, 4096, 128], P(None, 'dim'), may hold values from 0.1 to 2
- angle_state: float32 [5, 4096], P(None, 'dim'), may hold values from 0.1 to 2
Outputs:
- step_blocks: float32 [5, 4096, 128], P(None, 'dim')
- new_block_state: float32 [5, 4096, 128], P(None, 'dim')
- step_angles: float32 [5, 4096], P(None, 'dim')
- new_angle_state: float32 [5, 4096], P(None, 'dim')
The draws below stay inside these ranges and needn't reach their ends.
All inputs are finite; a program needn't handle non-finite values.
Results may differ from the reference program's by a relative error of at most 0.015.
The reference program's roundings to bfloat16 on the way count: a program that leaves them out, or rounds other values in their place, can miss the bound.
Values may be sent and summed in bfloat16 or wider, within the bound.
A program may use at most 128 MiB of HBM per device.

```python
import math
import jax
import jax.numpy as jnp
from jax import lax

D = 4096
BLOCK = 128
S = 5
LEVELS = 16
ROWS_DEV = 1664
ROWS = 53248
N_ROW = 32


def with_ends(entries, key, least, largest):
    index_at = [jax.random.randint(jax.random.fold_in(key, axis), (), 0, length) for axis, length in enumerate(entries.shape)]
    longest = entries.shape.index(max(entries.shape))
    next_to = index_at[:longest] + [(index_at[longest] + 1) % entries.shape[longest]] + index_at[longest + 1:]
    return entries.at[tuple(index_at)].set(least).at[tuple(next_to)].set(largest)


def block_levels(rng, shape, shards, smallest, top_value):
    level = 1.0
    for dim, shards_of in shards:
        heights = jax.random.uniform(jax.random.fold_in(jax.random.fold_in(rng, 6), dim), (shards_of,), jnp.float32, smallest / len(shards), top_value / len(shards))
        level = level * jnp.repeat(jnp.exp(heights), shape[dim] // shards_of).reshape((-1,) + (1,) * (len(shape) - 1 - dim))
    return level


def gaussian(own_key, shape, width, reach, cuts=(), kind=jnp.bfloat16):
    values = jax.random.normal(own_key, shape, jnp.float32) * width
    if len(cuts) > 0:
        values = block_levels(own_key, shape, cuts, -0.22, 0.18) * values
    return jnp.clip(values, min=-reach, max=reach).astype(kind)


def setup_inputs(seed: int = 0) -> dict:
    key_list = jax.random.split(jax.random.key(seed), 9)
    vectors = gaussian(key_list[0], (ROWS, D), 1.0, 6.0, ((0, 32), (1, 16)))
    blocks = gaussian(key_list[1], (S, D, BLOCK), BLOCK ** -0.5, 0.5, ((1, 16),), jnp.float32)
    angles = jnp.clip(jax.random.uniform(key_list[2], (S, D), jnp.float32, -3.140625, 3.140625), -3.140625, 3.140625)
    codes = with_ends(jax.random.randint(key_list[3], (ROWS, D), 0, 16), jax.random.fold_in(key_list[3], 1), 0, 15).astype(jnp.int32)
    scale_index = with_ends(jax.random.randint(key_list[4], (ROWS,), 0, LEVELS), jax.random.fold_in(key_list[4], 1), 0, LEVELS - 1).astype(jnp.int32)
    scale_table = jnp.clip(jnp.exp(jax.random.uniform(key_list[5], (LEVELS,), jnp.float32, math.log(0.05), math.log(0.3))), 0.05, 0.3)
    block_state = jnp.clip(jnp.exp(math.log(2.0) - 2.9957323 * jax.random.uniform(key_list[6], (S, D, BLOCK), jnp.float32) ** block_levels(key_list[6], (S, D, BLOCK), ((1, 16),), -0.2, 0.2)), 0.1, 2.0)
    angle_state = jnp.clip(jnp.exp(math.log(2.0) - 2.9957323 * jax.random.uniform(key_list[7], (S, D), jnp.float32) ** block_levels(key_list[7], (S, D), ((1, 16),), -0.2, 0.2)), 0.1, 2.0)
    return {"vectors": vectors, "blocks": blocks, "angles": angles, "codes": codes, "scale_index": scale_index, "scale_table": scale_table, "block_state": block_state, "angle_state": angle_state}


def swap_halves(tensor, section):
    layout = tensor.shape
    stride = 2 ** section
    number = layout[-2]
    parted = tensor.reshape(layout[:-2] + (number // (2 * stride), 2, stride, layout[-1]))
    return jnp.flip(parted, axis=-3).reshape(layout)

def reference(vectors, blocks, angles, codes, scale_index, scale_table, block_state, angle_state):
    block_count = D // BLOCK
    weights = blocks.astype(jnp.bfloat16).reshape(S, block_count, BLOCK, BLOCK)
    thetas = angles.reshape(S, block_count, BLOCK)
    cosines = jnp.cos(thetas)
    sines = jnp.sin(thetas)
    block_ids = jnp.arange(block_count, dtype=jnp.int32)
    all_signs = [jnp.where(block_ids // 2 ** section % 2 == 0, 1.0, -1.0).astype(jnp.float32)[:, None] for section in range(S)]

    def group(carry, inputs):
        rows_x, rows_codes, rows_index = inputs
        current = rows_x.reshape(ROWS_DEV, block_count, BLOCK)
        saved = []
        for section in range(S):
            mixed = jnp.einsum('rnb,nbc->rnc', current.astype(jnp.float32), weights[section].astype(jnp.float32)).astype(jnp.bfloat16)
            partner = swap_halves(mixed, section)
            result = (cosines[section] * mixed.astype(jnp.float32) + all_signs[section] * sines[section] * partner.astype(jnp.float32)).astype(jnp.bfloat16)
            saved.append((current, mixed, partner))
            current = result
        factor = scale_table[rows_index]
        recon = factor[:, None] * (rows_codes.astype(jnp.float32) - 7.5)
        cotangent = ((current.reshape(ROWS_DEV, D).astype(jnp.float32) - recon) / math.sqrt(ROWS)).astype(jnp.bfloat16).reshape(ROWS_DEV, block_count, BLOCK)
        block_grads = [None] * S
        angle_grads = [None] * S
        for section in reversed(range(S)):
            source, mixed, partner = saved[section]
            signs = all_signs[section]
            upstream = cotangent.astype(jnp.float32)
            angle_grads[section] = lax.optimization_barrier(jnp.sum(upstream * (-sines[section] * mixed.astype(jnp.float32) + signs * cosines[section] * partner.astype(jnp.float32)), axis=0))
            outgoing = (signs * sines[section] * upstream).astype(jnp.bfloat16)
            incoming = swap_halves(outgoing, section)
            direction = (cosines[section] * upstream + incoming.astype(jnp.float32)).astype(jnp.bfloat16)
            block_grads[section] = jnp.einsum('rnb,rnc->nbc', source.astype(jnp.float32), direction.astype(jnp.float32))
            if section > 0:
                cotangent = jnp.einsum('rnc,nbc->rnb', direction.astype(jnp.float32), weights[section].astype(jnp.float32)).astype(jnp.bfloat16)
        return ((carry[0] + jnp.stack(block_grads), carry[1] + jnp.stack(angle_grads)), None)
    start = (jnp.zeros((S, block_count, BLOCK, BLOCK), jnp.float32), jnp.zeros((S, block_count, BLOCK), jnp.float32))
    sliced = (vectors.reshape(N_ROW, ROWS_DEV, D), codes.reshape(N_ROW, ROWS_DEV, D), scale_index.reshape(N_ROW, ROWS_DEV))
    totals, _ = lax.scan(group, start, sliced)
    grad_blocks = totals[0].reshape(S, D, BLOCK)
    grad_angles = totals[1].reshape(S, D)
    new_block_state = 0.9 * block_state + 0.1 * grad_blocks * grad_blocks
    step_blocks = grad_blocks / jnp.sqrt(new_block_state)
    new_angle_state = 0.9 * angle_state + 0.1 * grad_angles * grad_angles
    step_angles = grad_angles / jnp.sqrt(new_angle_state)
    return (step_blocks, new_block_state, step_angles, new_angle_state)
```

```python
import math

import jax
import jax.numpy as jnp
from jax import lax
from jax.experimental import pallas as pl
from jax.experimental.pallas import tpu as pltpu
from jax.sharding import PartitionSpec as P

BLOCK = 128
S = 5
W = 256
R = 208
SUB = 16
XS = S * W // 4
ZS = XS // 4
MESH = pl.DeviceIdType.MESH
F32 = jnp.float32
BF16 = jnp.bfloat16


def flip(value, mask):
    for bit in (1, 2, 4, 8):
        if mask & bit:
            value = value + bit * (1 - 2 * ((value // bit) % 2))
    return value


def swap(value):
    return jnp.concatenate([value[:, BLOCK:], value[:, :BLOCK]], axis=1)


def fold(value):
    return jnp.sum(value.reshape(-1, 8, value.shape[-1]), axis=0)


def make_kernel(home_rows, total_rows):
    n = home_rows // R
    scale = 1.0 / math.sqrt(total_rows)

    def kernel(
        vec, codes, w, ang, idx, tab, grad_o, ang_o,
        u, v, vp, gs, qs, qp, dv, cod, codsend, wb, trig, fc, fac, acc, sa, sb,
        sx, rx, sxs, sz, rz, szs, sk, rk, gx,
        lsem, w_s, w_r, t_s, t_r, v_s, v_r, c_s, c_r, f_s, f_r, b_s, b_r, r_s, r_r,
    ):
        d = lax.axis_index("dim")
        r = lax.axis_index("row")
        zh, y, c = d // 8, (d // 2) % 4, d % 2
        x, zl = r // 8, r % 8
        kk, ii = zh * 2 + zl // 4, zl % 4

        def device(zh=zh, y=y, c=c, x=x, kk=None, ii=ii):
            lo = zl // 4
            if kk is not None:
                zh, lo = kk // 2, kk % 2
            return (zh * 8 + y * 2 + c, x * 8 + lo * 4 + ii)

        across = device(zh=1 - zh)
        core = device(c=1 - c)
        y_near, y_far = device(y=flip(y, 1)), device(y=flip(y, 2))
        x_peers = [device(x=flip(x, m)) for m in (1, 2, 3)]
        i_peers = [device(ii=flip(ii, m)) for m in (1, 2, 3)]
        k_peers = [device(kk=flip(kk, m)) for m in (1, 2, 3)]
        partners = [None, core, y_near, y_far]
        greeted = [core, y_near, y_far] + x_peers + i_peers + k_peers

        def remote(src, dst, send, recv, target):
            return pltpu.make_async_remote_copy(
                src_ref=src, dst_ref=dst, send_sem=send, recv_sem=recv,
                device_id=target, device_id_type=MESH,
            )

        barrier = pltpu.get_barrier_semaphore()
        for target in greeted:
            pl.semaphore_signal(barrier, inc=1, device_id=target, device_id_type=MESH)

        wb[0] = w[...].astype(BF16)
        lane = lax.broadcasted_iota(jnp.int32, (1, W), 1)
        bits = [jnp.where(lane < BLOCK, 1.0, -1.0).astype(F32)]
        for bit in (c, y % 2, y // 2, zh):
            bits.append(jnp.full((1, W), (1 - 2 * bit).astype(F32), F32))
        trig[0, 0:S] = jnp.cos(ang[...])
        sines = jnp.sin(ang[...])
        for s in range(S):
            trig[0, 8 + s : 9 + s] = bits[s] * sines[s : s + 1]
        acc[...] = jnp.zeros_like(acc)
        sa[...] = jnp.zeros_like(sa)
        sb[...] = jnp.zeros_like(sb)
        pl.semaphore_wait(barrier, len(greeted))

        home = pl.multiple_of(zh * home_rows, 64)
        away = pl.multiple_of((1 - zh) * home_rows, 64)

        def weight_copy(step):
            rows = pl.ds(pl.multiple_of(x * XS, 64), XS)
            if step == 0:
                return remote(wb.at[0, rows], wb.at[1, rows], w_s.at[0], w_r.at[0], across)
            return remote(
                wb.at[1, rows], wb.at[1, rows], w_s.at[step], w_r.at[step], x_peers[step - 1]
            )

        def trig_copy():
            return remote(trig.at[0], trig.at[1], t_s.at[0], t_r.at[0], across)

        def vec_copy(j):
            rows = pl.ds(pl.multiple_of(away + j * R, 16), R)
            return remote(vec.at[rows], u.at[0, n + j], v_s.at[j], v_r.at[j], across)

        def own_copy(j):
            rows = pl.ds(pl.multiple_of(home + j * R, 16), R)
            return pltpu.make_async_copy(vec.at[rows], u.at[0, j], lsem.at[j])

        def code_copy(j):
            return remote(codsend.at[j], cod.at[j], c_s.at[j], c_r.at[j], across)

        def fwd_copy(s, i):
            return remote(
                v.at[s, i], vp.at[s - 1, i], f_s.at[s - 1, i], f_r.at[s - 1, i], partners[s]
            )

        def bwd_copy(s, j):
            return remote(
                qs.at[s - 1, j], qp.at[s - 1, j], b_s.at[s - 1, j], b_r.at[s - 1, j], partners[s]
            )

        weight_copy(0).start()
        trig_copy().start()
        for j in range(n):
            own_copy(j).start()
        for j in range(n):
            vec_copy(j).start()

        def rows_of(k):
            return pl.ds(pl.multiple_of(k * SUB, SUB), SUB)

        for j in range(n):

            def convert(k, carry, j=j):
                rows = pl.ds(pl.multiple_of(away + j * R + k * SUB, 16), SUB)
                codsend[j, rows_of(k)] = codes[rows].astype(F32).astype(BF16)
                return carry

            lax.fori_loop(0, R // SUB, convert, 0)
            code_copy(j).start()
        index = idx[...]
        factor = jnp.zeros(index.shape, F32)
        for level in range(tab.shape[0]):
            factor = jnp.where(index == level, tab[level], factor)
        fc[0 : index.shape[0]] = factor

        def spread(p, carry):
            piece = zh * (home_rows // 64) + p
            row = fc[pl.ds(piece // 2, 1)]
            at = lax.broadcasted_iota(jnp.int32, (64, BLOCK), 1)
            want = lax.broadcasted_iota(jnp.int32, (64, BLOCK), 0) + 64 * (piece % 2)
            column = jnp.sum(jnp.where(at == want, row, 0.0), axis=1, keepdims=True)
            fac[pl.ds(pl.multiple_of(p * 64, 64), 64)] = jnp.broadcast_to(column, (64, BLOCK))
            return carry

        lax.fori_loop(0, home_rows // 64, spread, 0)

        def wrow(s, b):
            return pl.ds(s * W + b * BLOCK, BLOCK)

        def lanes(b):
            return pl.ds(b * BLOCK, BLOCK)

        def cos_of(h, s):
            return trig[h, pl.ds(s, 1)]

        def sin_of(h, s):
            return trig[h, pl.ds(8 + s, 1)]

        def mix(s, i, h):
            for b in range(2):
                v[s, i, :, lanes(b)] = jnp.dot(
                    u[s, i, :, lanes(b)], wb[h, wrow(s, b)], preferred_element_type=F32
                ).astype(BF16)

        def combine(s, i, h):
            cosine, sine = cos_of(h, s), sin_of(h, s)

            def step(k, carry):
                rows = rows_of(k)
                mine = v[s, i, rows].astype(F32)
                theirs = swap(mine) if s == 0 else vp[s - 1, i, rows].astype(F32)
                u[s + 1, i, rows] = (cosine * mine + sine * theirs).astype(BF16)
                return carry

            lax.fori_loop(0, R // SUB, step, 0)

        def forward(t, carry):
            for s in (3, 2, 1):
                i = t - s

                @pl.when((i >= 0) & (i < 2 * n))
                def _(s=s, i=i):
                    h = i // n
                    fwd_copy(s, i).wait_recv()
                    combine(s, i, h)
                    mix(s + 1, i, h)
                    if s < 3:
                        fwd_copy(s + 1, i).start()

            @pl.when(t == 2)
            def _():
                weight_copy(0).wait_recv()
                for step in (1, 2, 3):
                    weight_copy(step).start()

            @pl.when(t == n)
            def _():
                for step in (1, 2, 3):
                    weight_copy(step).wait_recv()
                trig_copy().wait_recv()

            @pl.when(t < n)
            def _():
                own_copy(t).wait()

            @pl.when((t >= n) & (t < 2 * n))
            def _():
                vec_copy(t - n).wait_recv()

            @pl.when(t < 2 * n)
            def _():
                h = t // n
                mix(0, t, h)
                combine(0, t, h)
                mix(1, t, h)
                fwd_copy(1, t).start()

            return carry

        lax.fori_loop(0, 2 * n + 3, forward, 0)

        def weight_grad(s, j):
            for h in range(2):
                for b in range(2):
                    acc[h, wrow(s, b)] += lax.dot_general(
                        u[s, h * n + j, :, lanes(b)],
                        dv[h, :, lanes(b)],
                        (((0,), (0,)), ((), ())),
                        preferred_element_type=F32,
                    )

        def pull(s, j):
            t = s - 1
            for h in range(2):
                i = h * n + j
                slot = max(t, 1) - 1
                for b in range(2):
                    gs[slot, j, h, :, lanes(b)] = lax.dot_general(
                        dv[h, :, lanes(b)],
                        wb[h, wrow(s, b)],
                        (((1,), (1,)), ((), ())),
                        preferred_element_type=F32,
                    ).astype(BF16)
            for h in range(2):
                i = h * n + j
                cosine, sine = cos_of(h, t), sin_of(h, t)

                def step(k, sums, h=h, i=i, cosine=cosine, sine=sine):
                    rows = rows_of(k)
                    up = gs[slot, j, h, rows].astype(F32)
                    mine = v[t, i, rows].astype(F32)
                    theirs = swap(mine) if t == 0 else vp[t - 1, i, rows].astype(F32)
                    sent = (sine * up).astype(BF16)
                    if t == 0:
                        dv[h, rows] = (cosine * up + swap(sent.astype(F32))).astype(BF16)
                    else:
                        qs[t - 1, j, h, rows] = sent
                    return sums[0] + fold(up * mine), sums[1] + fold(up * theirs)

                one, two = lax.fori_loop(0, R // SUB, step, (sa[h, t], sb[h, t]))
                sa[h, t] = one
                sb[h, t] = two

        def turn(j):
            code_copy(j).wait_recv()
            cos_a, sin_a, cos_b, sin_b = cos_of(0, 4), sin_of(0, 4), cos_of(1, 4), sin_of(1, 4)

            def step(k, sums):
                rows = rows_of(k)
                va, vb = v[4, j, rows].astype(F32), v[4, n + j, rows].astype(F32)
                f = fac[pl.ds(pl.multiple_of(j * R + k * SUB, 16), SUB)]
                f = jnp.concatenate([f, f], axis=1)
                own = codes[pl.ds(pl.multiple_of(home + j * R + k * SUB, 16), SUB)].astype(F32)
                recon_a = f * (own - 7.5)
                recon_b = f * (cod[j, rows].astype(F32) - 7.5)
                ua = (cos_a * va + sin_a * vb).astype(BF16).astype(F32)
                ub = (cos_b * vb + sin_b * va).astype(BF16).astype(F32)
                ga = ((ua - recon_a) * scale).astype(BF16).astype(F32)
                gb = ((ub - recon_b) * scale).astype(BF16).astype(F32)
                qa = (sin_a * ga).astype(BF16).astype(F32)
                qb = (sin_b * gb).astype(BF16).astype(F32)
                dv[0, rows] = (cos_a * ga + qb).astype(BF16)
                dv[1, rows] = (cos_b * gb + qa).astype(BF16)
                return (
                    sums[0] + fold(ga * va),
                    sums[1] + fold(ga * vb),
                    sums[2] + fold(gb * vb),
                    sums[3] + fold(gb * va),
                )

            sums = lax.fori_loop(0, R // SUB, step, (sa[0, 4], sb[0, 4], sa[1, 4], sb[1, 4]))
            sa[0, 4], sb[0, 4], sa[1, 4], sb[1, 4] = sums
            weight_grad(4, j)
            pull(4, j)
            bwd_copy(3, j).start()

        def back(s, j):
            bwd_copy(s, j).wait_recv()
            for h in range(2):
                cosine = cos_of(h, s)

                def step(k, carry, h=h, cosine=cosine):
                    rows = rows_of(k)
                    up = gs[s - 1, j, h, rows].astype(F32)
                    dv[h, rows] = (cosine * up + qp[s - 1, j, h, rows].astype(F32)).astype(BF16)
                    return carry

                lax.fori_loop(0, R // SUB, step, 0)
            weight_grad(s, j)
            pull(s, j)
            if s > 1:
                bwd_copy(s - 1, j).start()
            else:
                weight_grad(0, j)

        def backward(t, carry):
            for s in (1, 2, 3):
                j = t - (4 - s)

                @pl.when((j >= 0) & (j < n))
                def _(s=s, j=j):
                    back(s, j)

            @pl.when(t < n)
            def _():
                turn(t)

            return carry

        lax.fori_loop(0, n + 3, backward, 0)

        turned = []
        for h in range(2):
            parts = []
            for s in range(S):
                a = jnp.sum(sa[h, s], axis=0, keepdims=True)
                b = jnp.sum(sb[h, s], axis=0, keepdims=True)
                sign = bits[s] if (h == 0 or s < 4) else -bits[s]
                whole = sign * (cos_of(h, s) * b - sin_of(h, s) * a)
                parts += [whole[:, :BLOCK], whole[:, BLOCK:]]
            parts.append(jnp.zeros((6, BLOCK), F32))
            turned.append(jnp.concatenate(parts, axis=0).astype(BF16))
        angles = jnp.concatenate(turned, axis=0)

        def fill_x(ref, p):
            for h in range(2):
                ref[pl.ds(h * XS, XS)] = acc[h, pl.ds(pl.multiple_of(p * XS, 64), XS)].astype(BF16)
            ref[pl.ds(2 * XS, 32)] = angles

        def x_copy(m):
            return remote(sx.at[m], rx.at[x], r_s.at[m], r_r.at[m], x_peers[m])

        def i_copy(m):
            return remote(sz.at[m], rz.at[ii], r_s.at[3 + m], r_r.at[3 + m], i_peers[m])

        def k_copy(m):
            return remote(sk.at[m], rk.at[kk], r_s.at[6 + m], r_r.at[6 + m], k_peers[m])

        def gi_copy(m):
            rows = pl.ds(pl.multiple_of(ii * ZS, 16), ZS)
            return remote(
                gx.at[x, rows], gx.at[x, rows], r_s.at[9 + m], r_r.at[9 + m], i_peers[m]
            )

        def gx_copy(m):
            return remote(gx.at[x], gx.at[x], r_s.at[12 + m], r_r.at[12 + m], x_peers[m])

        for m in range(3):
            fill_x(sx.at[m], flip(x, m + 1))
            x_copy(m).start()
        fill_x(rx.at[x], x)
        for m in range(3):
            x_copy(m).wait_recv()
        sxs[...] = (rx[0].astype(F32) + rx[1].astype(F32)) + (rx[2].astype(F32) + rx[3].astype(F32))

        def fill_z(ref, p):
            for h in range(2):
                ref[pl.ds(h * ZS, ZS)] = sxs[
                    pl.ds(pl.multiple_of(h * XS + p * ZS, 16), ZS)
                ].astype(BF16)
            ref[pl.ds(2 * ZS, 32)] = sxs[pl.ds(2 * XS, 32)].astype(BF16)

        for m in range(3):
            fill_z(sz.at[m], flip(ii, m + 1))
            i_copy(m).start()
        fill_z(rz.at[ii], ii)
        for m in range(3):
            i_copy(m).wait_recv()
        szs[...] = (rz[0].astype(F32) + rz[1].astype(F32)) + (rz[2].astype(F32) + rz[3].astype(F32))

        def fill_k(ref, h):
            ref[pl.ds(0, ZS)] = szs[pl.ds(h * ZS, ZS)].astype(BF16)
            ref[pl.ds(ZS, 16)] = szs[pl.ds(2 * ZS + h * 16, 16)].astype(BF16)

        for m in range(3):
            fill_k(sk.at[m], 0 if m == 0 else 1)
            k_copy(m).start()
        fill_k(rk.at[kk], 0)
        for m in range(3):
            k_copy(m).wait_recv()
        final = (rk[0].astype(F32) + rk[1].astype(F32)) + (rk[2].astype(F32) + rk[3].astype(F32))
        ang_o[...] = final[ZS:]
        gx[x, pl.ds(pl.multiple_of(ii * ZS, 16), ZS)] = final[:ZS].astype(BF16)

        for m in range(3):
            gi_copy(m).start()
        for m in range(3):
            gi_copy(m).wait_recv()
        for m in range(3):
            gx_copy(m).start()
        for m in range(3):
            gx_copy(m).wait_recv()
        for p in range(4):
            grad_o[pl.ds(p * XS, XS)] = gx[p].astype(F32)

        for step in range(4):
            weight_copy(step).wait_send()
        trig_copy().wait_send()

        def drain(j, carry):
            vec_copy(j).wait_send()
            code_copy(j).wait_send()
            for s in (1, 2, 3):
                fwd_copy(s, j).wait_send()
                fwd_copy(s, n + j).wait_send()
                bwd_copy(s, j).wait_send()
            return carry

        lax.fori_loop(0, n, drain, 0)
        for m in range(3):
            for copy in (x_copy, i_copy, k_copy, gi_copy, gx_copy):
                copy(m).wait_send()

    return kernel, n


def gradients(vectors, blocks, angles, codes, scale_index, scale_table):
    num_rows = vectors.shape[0]
    kernel, n = make_kernel(num_rows // 2, num_rows * 32)
    vmem = pl.BlockSpec(memory_space=pltpu.VMEM)
    dma = pltpu.SemaphoreType.DMA
    shapes = [
        pltpu.VMEM((S, 2 * n, R, W), BF16),
        pltpu.VMEM((S, 2 * n, R, W), BF16),
        pltpu.VMEM((3, 2 * n, R, W), BF16),
        pltpu.VMEM((3, n, 2, R, W), BF16),
        pltpu.VMEM((3, n, 2, R, W), BF16),
        pltpu.VMEM((3, n, 2, R, W), BF16),
        pltpu.VMEM((2, R, W), BF16),
        pltpu.VMEM((n, R, W), BF16),
        pltpu.VMEM((n, R, W), BF16),
        pltpu.VMEM((2, S * W, BLOCK), BF16),
        pltpu.VMEM((2, 16, W), F32),
        pltpu.VMEM((16, BLOCK), F32),
        pltpu.VMEM((num_rows // 2, BLOCK), F32),
        pltpu.VMEM((2, S * W, BLOCK), F32),
        pltpu.VMEM((2, S, 8, W), F32),
        pltpu.VMEM((2, S, 8, W), F32),
        pltpu.VMEM((3, 2 * XS + 32, BLOCK), BF16),
        pltpu.VMEM((4, 2 * XS + 32, BLOCK), BF16),
        pltpu.VMEM((2 * XS + 32, BLOCK), F32),
        pltpu.VMEM((3, 2 * ZS + 32, BLOCK), BF16),
        pltpu.VMEM((4, 2 * ZS + 32, BLOCK), BF16),
        pltpu.VMEM((2 * ZS + 32, BLOCK), F32),
        pltpu.VMEM((3, ZS + 16, BLOCK), BF16),
        pltpu.VMEM((4, ZS + 16, BLOCK), BF16),
        pltpu.VMEM((4, XS, BLOCK), BF16),
        dma((n,)),
        dma((4,)), dma((4,)), dma((1,)), dma((1,)), dma((n,)), dma((n,)), dma((n,)), dma((n,)),
        dma((3, 2 * n)), dma((3, 2 * n)), dma((3, n)), dma((3, n)), dma((15,)), dma((15,)),
    ]
    return pl.pallas_call(
        kernel,
        name="butterfly",
        out_shape=(
            jax.ShapeDtypeStruct((S * W, BLOCK), F32),
            jax.ShapeDtypeStruct((16, BLOCK), F32),
        ),
        in_specs=[
            pl.BlockSpec(memory_space=pl.ANY),
            vmem, vmem, vmem, vmem,
            pl.BlockSpec(memory_space=pltpu.SMEM),
        ],
        out_specs=(vmem, vmem),
        scratch_shapes=shapes,
        compiler_params=pltpu.CompilerParams(
            collective_id=0, has_side_effects=True, vmem_limit_bytes=56 * 2**20
        ),
    )(
        vectors, codes, blocks.reshape(S * W, BLOCK), angles,
        scale_index.reshape(num_rows // BLOCK, BLOCK), scale_table,
    )


def local(vectors, blocks, angles, codes, scale_index, scale_table, block_state, angle_state):
    grad, turned = gradients(vectors, blocks, angles, codes, scale_index, scale_table)
    grad_blocks = grad.reshape(S, W, BLOCK)
    grad_angles = turned[: 2 * S].reshape(S, W)
    new_block_state = 0.9 * block_state + 0.1 * grad_blocks * grad_blocks
    step_blocks = grad_blocks / jnp.sqrt(new_block_state)
    new_angle_state = 0.9 * angle_state + 0.1 * grad_angles * grad_angles
    step_angles = grad_angles / jnp.sqrt(new_angle_state)
    return (step_blocks, new_block_state, step_angles, new_angle_state)


def solution(mesh):
    in_specs = (
        P("row", "dim"),
        P(None, "dim", None),
        P(None, "dim"),
        P("row", "dim"),
        P("row"),
        P(),
        P(None, "dim", None),
        P(None, "dim"),
    )
    out_specs = (P(None, "dim", None), P(None, "dim", None), P(None, "dim"), P(None, "dim"))
    return jax.shard_map(local, mesh=mesh, in_specs=in_specs, out_specs=out_specs, check_vma=False)
```

```python
import math

import jax
import jax.numpy as jnp
from jax import lax
from jax.experimental import pallas as pl
from jax.experimental.pallas import tpu as pltpu
from jax.sharding import PartitionSpec as P

BLOCK = 128
S = 5
W = 256
R = 64
SUB = 16
XS = S * W // 4
ZS = XS // 4
XP = W // 4
ZP = XP // 4
AHEAD = 6
WINDOW = 4
LAG = 9
MESH = pl.DeviceIdType.MESH
F32 = jnp.float32
BF16 = jnp.bfloat16


def flip(value, mask):
    for bit in (1, 2, 4, 8):
        if mask & bit:
            value = value + bit * (1 - 2 * ((value // bit) % 2))
    return value


def swap(value):
    return jnp.concatenate([value[:, BLOCK:], value[:, :BLOCK]], axis=1)


def fold(value):
    return jnp.sum(value.reshape(-1, 8, value.shape[-1]), axis=0)


def make_kernel(home_rows, total_rows):
    n = home_rows // R
    scale = 1.0 / math.sqrt(total_rows)

    def kernel(
        vec, codes, w, ang, idx, tab, grad_o, ang_o,
        u, v, vp, gs, qs, qp, dv, cod, codsend, wb, trig, ang2, fc, fac, acc, sa, sb,
        sx, rx, sxs, sz, rz, szs, sk, rk, gx,
        lsem, w_s, w_r, t_s, t_r, v_s, v_r, c_s, c_r, f_s, f_r, b_s, b_r, r_s, r_r,
    ):
        d = lax.axis_index("dim")
        r = lax.axis_index("row")
        zh, y, c = d // 8, (d // 2) % 4, d % 2
        x, zl = r // 8, r % 8
        kk, ii = zh * 2 + zl // 4, zl % 4

        def device(zh=zh, y=y, c=c, x=x, kk=None, ii=ii):
            lo = zl // 4
            if kk is not None:
                zh, lo = kk // 2, kk % 2
            return (zh * 8 + y * 2 + c, x * 8 + lo * 4 + ii)

        across = device(zh=1 - zh)
        core = device(c=1 - c)
        y_near, y_far = device(y=flip(y, 1)), device(y=flip(y, 2))
        x_peers = [device(x=flip(x, m)) for m in (1, 2, 3)]
        i_peers = [device(ii=flip(ii, m)) for m in (1, 2, 3)]
        k_peers = [device(kk=flip(kk, m)) for m in (1, 2, 3)]
        partners = [None, core, y_near, y_far]
        greeted = [core, y_near, y_far] + x_peers + i_peers + k_peers

        def remote(src, dst, send, recv, target):
            return pltpu.make_async_remote_copy(
                src_ref=src, dst_ref=dst, send_sem=send, recv_sem=recv,
                device_id=target, device_id_type=MESH,
            )

        barrier = pltpu.get_barrier_semaphore()
        for target in greeted:
            pl.semaphore_signal(barrier, inc=1, device_id=target, device_id_type=MESH)

        wb[0] = w[...].astype(BF16)
        pl.semaphore_wait(barrier, len(greeted))

        home = pl.multiple_of(zh * home_rows, 64)
        away = pl.multiple_of((1 - zh) * home_rows, 64)

        def weight_copy(step):
            whole = pl.ds(pl.multiple_of(x * XS, 64), XS)
            piece = pl.ds(pl.multiple_of(x * XS + ii * ZS, 16), ZS)
            if step == 0:
                source, rows, target = 0, piece, across
            elif step < 4:
                source, rows, target = 1, piece, i_peers[step - 1]
            else:
                source, rows, target = 1, whole, x_peers[step - 4]
            return remote(wb.at[source, rows], wb.at[1, rows], w_s.at[step], w_r.at[step], target)

        def angle_copy():
            return remote(ang, ang2, t_s.at[0], t_r.at[0], across)

        def vec_copy(j):
            rows = pl.ds(pl.multiple_of(away + j * R, 16), R)
            return remote(vec.at[rows], u.at[0, n + j], v_s.at[j], v_r.at[j], across)

        def own_copy(j):
            rows = pl.ds(pl.multiple_of(home + j * R, 16), R)
            return pltpu.make_async_copy(vec.at[rows], u.at[0, j], lsem.at[j])

        def code_copy(j):
            return remote(codsend.at[j], cod.at[j], c_s.at[j], c_r.at[j], across)

        def fwd_copy(s, i):
            return remote(
                v.at[s, i], vp.at[s - 1, i], f_s.at[s - 1, i], f_r.at[s - 1, i], partners[s]
            )

        def bwd_copy(s, j):
            return remote(
                qs.at[s - 1, j], qp.at[s - 1, j], b_s.at[s - 1, j], b_r.at[s - 1, j], partners[s]
            )

        vec_copy(0).start()
        weight_copy(0).start()
        angle_copy().start()
        for j in range(n):
            own_copy(j).start()

        def steps(step, carry=None):
            for k in range(R // SUB):
                carry = step(k, carry)
            return carry

        def rows_of(k):
            return pl.ds(k * SUB, SUB)

        def send_codes(j):
            def step(k, carry):
                rows = pl.ds(pl.multiple_of(away + j * R + k * SUB, 16), SUB)
                codsend[j, rows_of(k)] = codes[rows].astype(F32).astype(BF16)

            steps(step)
            code_copy(j).start()

        for j in range(1, WINDOW):
            vec_copy(j).start()

        lane = lax.broadcasted_iota(jnp.int32, (1, W), 1)
        bits = [jnp.where(lane < BLOCK, 1.0, -1.0).astype(F32)]
        for bit in (c, y % 2, y // 2, zh):
            bits.append(jnp.full((1, W), (1 - 2 * bit).astype(F32), F32))

        def twiddle(h, theta):
            trig[h, 0:S] = jnp.cos(theta)
            sines = jnp.sin(theta)
            for s in range(S):
                sign = bits[s] if (h == 0 or s < 4) else -bits[s]
                trig[h, 8 + s : 9 + s] = sign * sines[s : s + 1]

        twiddle(0, ang[...])
        acc[...] = jnp.zeros_like(acc)
        sa[...] = jnp.zeros_like(sa)
        sb[...] = jnp.zeros_like(sb)
        index = idx[...]
        factor = jnp.zeros(index.shape, F32)
        for level in range(tab.shape[0]):
            factor = jnp.where(index == level, tab[level], factor)
        fc[0 : index.shape[0]] = factor

        def spread(p, carry):
            piece = zh * (home_rows // 64) + p
            row = fc[pl.ds(piece // 2, 1)]
            at = lax.broadcasted_iota(jnp.int32, (64, BLOCK), 1)
            want = lax.broadcasted_iota(jnp.int32, (64, BLOCK), 0) + 64 * (piece % 2)
            column = jnp.sum(jnp.where(at == want, row, 0.0), axis=1, keepdims=True)
            fac[pl.ds(pl.multiple_of(p * 64, 64), 64)] = jnp.broadcast_to(column, (64, BLOCK))
            return carry

        lax.fori_loop(0, home_rows // 64, spread, 0)

        def wrow(s, b):
            return pl.ds(s * W + b * BLOCK, BLOCK)

        def lanes(b):
            return pl.ds(b * BLOCK, BLOCK)

        def cos_of(h, s):
            return trig[h, pl.ds(s, 1)]

        def sin_of(h, s):
            return trig[h, pl.ds(8 + s, 1)]

        def mix(s, i, h):
            for b in range(2):
                v[s, i, :, lanes(b)] = jnp.dot(
                    u[s, i, :, lanes(b)], wb[h, wrow(s, b)], preferred_element_type=F32
                ).astype(BF16)

        def combine(s, i, h):
            cosine, sine = cos_of(h, s), sin_of(h, s)

            def step(k, carry):
                rows = rows_of(k)
                mine = v[s, i, rows].astype(F32)
                theirs = swap(mine) if s == 0 else vp[s - 1, i, rows].astype(F32)
                u[s + 1, i, rows] = (cosine * mine + sine * theirs).astype(BF16)

            steps(step)

        def start(i, h):
            mix(0, i, h)
            combine(0, i, h)
            mix(1, i, h)
            fwd_copy(1, i).start()

        def carry_on(s, i, h):
            fwd_copy(s, i).wait_recv()
            combine(s, i, h)
            mix(s + 1, i, h)
            if s < 3:
                fwd_copy(s + 1, i).start()

        def weight_grad(s, j):
            for h in range(2):
                for b in range(2):
                    acc[h, wrow(s, b)] += lax.dot_general(
                        u[s, h * n + j, :, lanes(b)],
                        dv[h, :, lanes(b)],
                        (((0,), (0,)), ((), ())),
                        preferred_element_type=F32,
                    )

        def pull(s, j):
            t = s - 1
            for h in range(2):
                i = h * n + j
                slot = max(t, 1) - 1
                for b in range(2):
                    gs[slot, j, h, :, lanes(b)] = lax.dot_general(
                        dv[h, :, lanes(b)],
                        wb[h, wrow(s, b)],
                        (((1,), (1,)), ((), ())),
                        preferred_element_type=F32,
                    ).astype(BF16)
            for h in range(2):
                i = h * n + j
                cosine, sine = cos_of(h, t), sin_of(h, t)

                def step(k, sums, h=h, i=i, cosine=cosine, sine=sine):
                    rows = rows_of(k)
                    up = gs[slot, j, h, rows].astype(F32)
                    mine = v[t, i, rows].astype(F32)
                    theirs = swap(mine) if t == 0 else vp[t - 1, i, rows].astype(F32)
                    sent = (sine * up).astype(BF16)
                    if t == 0:
                        dv[h, rows] = (cosine * up + swap(sent.astype(F32))).astype(BF16)
                    else:
                        qs[t - 1, j, h, rows] = sent
                    return sums[0] + fold(up * mine), sums[1] + fold(up * theirs)

                one, two = steps(step, (sa[h, t], sb[h, t]))
                sa[h, t] = one
                sb[h, t] = two

        def turn(j):
            code_copy(j).wait_recv()
            cos_a, sin_a, cos_b, sin_b = cos_of(0, 4), sin_of(0, 4), cos_of(1, 4), sin_of(1, 4)

            def step(k, sums):
                rows = rows_of(k)
                va, vb = v[4, j, rows].astype(F32), v[4, n + j, rows].astype(F32)
                f = fac[pl.ds(pl.multiple_of(j * R + k * SUB, 16), SUB)]
                f = jnp.concatenate([f, f], axis=1)
                own = codes[pl.ds(pl.multiple_of(home + j * R + k * SUB, 16), SUB)].astype(F32)
                recon_a = f * (own - 7.5)
                recon_b = f * (cod[j, rows].astype(F32) - 7.5)
                ua = (cos_a * va + sin_a * vb).astype(BF16).astype(F32)
                ub = (cos_b * vb + sin_b * va).astype(BF16).astype(F32)
                ga = ((ua - recon_a) * scale).astype(BF16).astype(F32)
                gb = ((ub - recon_b) * scale).astype(BF16).astype(F32)
                qa = (sin_a * ga).astype(BF16).astype(F32)
                qb = (sin_b * gb).astype(BF16).astype(F32)
                dv[0, rows] = (cos_a * ga + qb).astype(BF16)
                dv[1, rows] = (cos_b * gb + qa).astype(BF16)
                return (
                    sums[0] + fold(ga * va),
                    sums[1] + fold(ga * vb),
                    sums[2] + fold(gb * vb),
                    sums[3] + fold(gb * va),
                )

            sums = steps(step, (sa[0, 4], sb[0, 4], sa[1, 4], sb[1, 4]))
            sa[0, 4], sb[0, 4], sa[1, 4], sb[1, 4] = sums
            weight_grad(4, j)
            pull(4, j)
            bwd_copy(3, j).start()

        def back(s, j):
            bwd_copy(s, j).wait_recv()
            for h in range(2):
                cosine = cos_of(h, s)

                def step(k, carry, h=h, cosine=cosine):
                    rows = rows_of(k)
                    up = gs[s - 1, j, h, rows].astype(F32)
                    dv[h, rows] = (cosine * up + qp[s - 1, j, h, rows].astype(F32)).astype(BF16)

                steps(step)
            weight_grad(s, j)
            pull(s, j)
            if s > 1:
                bwd_copy(s - 1, j).start()
            else:
                weight_grad(0, j)

        def x_rows(s):
            return pl.ds((S - 1 - s) * 2 * XP, 2 * XP + (32 if s == 0 else 0))

        def x_copy(s, m):
            rows = x_rows(s)
            at = 3 * s + m
            return remote(sx.at[m, rows], rx.at[x, rows], r_s.at[at], r_r.at[at], x_peers[m])

        def x_fill(ref, s, p, angles):
            first = (S - 1 - s) * 2 * XP
            for h in range(2):
                rows = pl.ds(pl.multiple_of(s * W + p * XP, 64), XP)
                ref[pl.ds(first + h * XP, XP)] = acc[h, rows].astype(BF16)
            if s == 0:
                ref[pl.ds(first + 2 * XP, 32)] = angles

        def x_begin(s, angles=None):
            for m in range(3):
                x_fill(sx.at[m], s, flip(x, m + 1), angles)
                x_copy(s, m).start()
            x_fill(rx.at[x], s, x, angles)

        def one_loop(t, carry):
            def at_chunk(offset, last, body):
                j = t - offset

                @pl.when((j >= 0) & (j < n))
                def _():
                    body(j)

                for s in last:

                    @pl.when(j == n - 1)
                    def _(s=s):
                        x_begin(s)

            at_chunk(LAG + 11, (1,), lambda j: back(1, j))
            at_chunk(LAG + 10, (2,), lambda j: back(2, j))
            at_chunk(LAG + 8, (3,), lambda j: back(3, j))
            at_chunk(LAG + 5, (), lambda j: carry_on(3, n + j, 1))
            at_chunk(LAG + 3, (), lambda j: carry_on(2, n + j, 1))
            at_chunk(LAG + 1, (), lambda j: carry_on(1, n + j, 1))
            at_chunk(8, (), lambda j: carry_on(3, j, 0))
            at_chunk(5, (), lambda j: carry_on(2, j, 0))
            at_chunk(2, (), lambda j: carry_on(1, j, 0))

            @pl.when(t == 6)
            def _():
                weight_copy(0).wait_recv()
                for step in (1, 2, 3):
                    weight_copy(step).start()

            @pl.when(t == 8)
            def _():
                for step in (1, 2, 3):
                    weight_copy(step).wait_recv()
                for step in (4, 5, 6):
                    weight_copy(step).start()

            @pl.when(t == LAG)
            def _():
                angle_copy().wait_recv()
                twiddle(1, ang2[...])
                for step in (4, 5, 6):
                    weight_copy(step).wait_recv()

            @pl.when(t < n)
            def _():
                own_copy(t).wait()
                start(t, 0)

            def begin(j):
                vec_copy(j).wait_recv()

                @pl.when(j + WINDOW < n)
                def _():
                    vec_copy(j + WINDOW).start()

                start(n + j, 1)

            at_chunk(LAG, (), begin)
            at_chunk(LAG + 2, (), send_codes)
            at_chunk(LAG + AHEAD, (4,), turn)
            return carry

        lax.fori_loop(0, n + LAG + 11, one_loop, 0)

        turned = []
        for h in range(2):
            parts = []
            for s in range(S):
                a = jnp.sum(sa[h, s], axis=0, keepdims=True)
                b = jnp.sum(sb[h, s], axis=0, keepdims=True)
                sign = bits[s] if (h == 0 or s < 4) else -bits[s]
                whole = sign * (cos_of(h, s) * b - sin_of(h, s) * a)
                parts += [whole[:, :BLOCK], whole[:, BLOCK:]]
            parts.append(jnp.zeros((6, BLOCK), F32))
            turned.append(jnp.concatenate(parts, axis=0).astype(BF16))
        angles = jnp.concatenate(turned, axis=0)

        def z_copy(stage, m):
            at = 3 * (S + stage) + m
            piece = pl.ds(pl.multiple_of(ii * ZS, 16), ZS)
            source, target, peer = (
                (sz.at[m], rz.at[ii], i_peers[m]),
                (sk.at[m], rk.at[kk], k_peers[m]),
                (gx.at[x, piece], gx.at[x, piece], i_peers[m]),
                (gx.at[x], gx.at[x], x_peers[m]),
            )[stage]
            return remote(source, target, r_s.at[at], r_r.at[at], peer)

        def total(ref):
            return (ref[0].astype(F32) + ref[1].astype(F32)) + (
                ref[2].astype(F32) + ref[3].astype(F32)
            )

        def z_fill(ref, p):
            for h in range(2):
                for s in range(S):
                    first = (S - 1 - s) * 2 * XP + h * XP
                    rows = pl.ds(pl.multiple_of(first + p * ZP, 16), ZP)
                    ref[pl.ds((h * S + s) * ZP, ZP)] = sxs[rows].astype(BF16)
            ref[pl.ds(2 * ZS, 32)] = sxs[pl.ds(2 * XS, 32)].astype(BF16)

        def k_fill(ref, h):
            ref[pl.ds(0, ZS)] = szs[pl.ds(h * ZS, ZS)].astype(BF16)
            ref[pl.ds(ZS, 16)] = szs[pl.ds(2 * ZS + h * 16, 16)].astype(BF16)

        x_begin(0, angles)
        for s in reversed(range(S)):
            for m in range(3):
                x_copy(s, m).wait_recv()
        sxs[...] = total(rx)
        for m in range(3):
            z_fill(sz.at[m], flip(ii, m + 1))
            z_copy(0, m).start()
        z_fill(rz.at[ii], ii)
        for m in range(3):
            z_copy(0, m).wait_recv()
        szs[...] = total(rz)
        for m in range(3):
            k_fill(sk.at[m], 0 if m == 0 else 1)
            z_copy(1, m).start()
        k_fill(rk.at[kk], 0)
        for m in range(3):
            z_copy(1, m).wait_recv()
        final = total(rk)
        gx[x, pl.ds(pl.multiple_of(ii * ZS, 16), ZS)] = final[:ZS].astype(BF16)
        for m in range(3):
            z_copy(2, m).start()
        ang_o[...] = final[ZS:]
        for m in range(3):
            z_copy(2, m).wait_recv()
        for m in range(3):
            z_copy(3, m).start()
        for m in range(3):
            z_copy(3, m).wait_recv()
        for p in range(4):
            for q in range(4):
                for s in range(S):
                    grad_o[pl.ds(s * W + p * XP + q * ZP, ZP)] = gx[
                        p, pl.ds(q * ZS + s * ZP, ZP)
                    ].astype(F32)

        for step in range(7):
            weight_copy(step).wait_send()
        angle_copy().wait_send()

        def drain(j, carry):
            vec_copy(j).wait_send()
            code_copy(j).wait_send()
            for s in (1, 2, 3):
                fwd_copy(s, j).wait_send()
                fwd_copy(s, n + j).wait_send()
                bwd_copy(s, j).wait_send()
            return carry

        lax.fori_loop(0, n, drain, 0)
        for m in range(3):
            for s in range(S):
                x_copy(s, m).wait_send()
            for stage in range(4):
                z_copy(stage, m).wait_send()

    return kernel, n


def gradients(vectors, blocks, angles, codes, scale_index, scale_table):
    num_rows = vectors.shape[0]
    kernel, n = make_kernel(num_rows // 2, num_rows * 32)
    vmem = pl.BlockSpec(memory_space=pltpu.VMEM)
    dma = pltpu.SemaphoreType.DMA
    shapes = [
        pltpu.VMEM((S, 2 * n, R, W), BF16),
        pltpu.VMEM((S, 2 * n, R, W), BF16),
        pltpu.VMEM((3, 2 * n, R, W), BF16),
        pltpu.VMEM((3, n, 2, R, W), BF16),
        pltpu.VMEM((3, n, 2, R, W), BF16),
        pltpu.VMEM((3, n, 2, R, W), BF16),
        pltpu.VMEM((2, R, W), BF16),
        pltpu.VMEM((n, R, W), BF16),
        pltpu.VMEM((n, R, W), BF16),
        pltpu.VMEM((2, S * W, BLOCK), BF16),
        pltpu.VMEM((2, 16, W), F32),
        pltpu.VMEM((S, W), F32),
        pltpu.VMEM((16, BLOCK), F32),
        pltpu.VMEM((num_rows // 2, BLOCK), F32),
        pltpu.VMEM((2, S * W, BLOCK), F32),
        pltpu.VMEM((2, S, 8, W), F32),
        pltpu.VMEM((2, S, 8, W), F32),
        pltpu.VMEM((3, 2 * XS + 32, BLOCK), BF16),
        pltpu.VMEM((4, 2 * XS + 32, BLOCK), BF16),
        pltpu.VMEM((2 * XS + 32, BLOCK), F32),
        pltpu.VMEM((3, 2 * ZS + 32, BLOCK), BF16),
        pltpu.VMEM((4, 2 * ZS + 32, BLOCK), BF16),
        pltpu.VMEM((2 * ZS + 32, BLOCK), F32),
        pltpu.VMEM((3, ZS + 16, BLOCK), BF16),
        pltpu.VMEM((4, ZS + 16, BLOCK), BF16),
        pltpu.VMEM((4, XS, BLOCK), BF16),
        dma((n,)),
        dma((7,)), dma((7,)), dma((1,)), dma((1,)), dma((n,)), dma((n,)), dma((n,)), dma((n,)),
        dma((3, 2 * n)), dma((3, 2 * n)), dma((3, n)), dma((3, n)),
        dma((27,)), dma((27,)),
    ]
    return pl.pallas_call(
        kernel,
        name="butterfly",
        out_shape=(
            jax.ShapeDtypeStruct((S * W, BLOCK), F32),
            jax.ShapeDtypeStruct((16, BLOCK), F32),
        ),
        in_specs=[
            pl.BlockSpec(memory_space=pl.ANY),
            vmem, vmem, vmem, vmem,
            pl.BlockSpec(memory_space=pltpu.SMEM),
        ],
        out_specs=(vmem, vmem),
        scratch_shapes=shapes,
        compiler_params=pltpu.CompilerParams(
            collective_id=0, has_side_effects=True, vmem_limit_bytes=56 * 2**20
        ),
    )(
        vectors, codes, blocks.reshape(S * W, BLOCK), angles,
        scale_index.reshape(num_rows // BLOCK, BLOCK), scale_table,
    )


def local(vectors, blocks, angles, codes, scale_index, scale_table, block_state, angle_state):
    grad, turned = gradients(vectors, blocks, angles, codes, scale_index, scale_table)
    grad_blocks = grad.reshape(S, W, BLOCK)
    grad_angles = turned[: 2 * S].reshape(S, W)
    new_block_state = 0.9 * block_state + 0.1 * grad_blocks * grad_blocks
    step_blocks = grad_blocks / jnp.sqrt(new_block_state)
    new_angle_state = 0.9 * angle_state + 0.1 * grad_angles * grad_angles
    step_angles = grad_angles / jnp.sqrt(new_angle_state)
    return (step_blocks, new_block_state, step_angles, new_angle_state)


def solution(mesh):
    in_specs = (
        P("row", "dim"),
        P(None, "dim", None),
        P(None, "dim"),
        P("row", "dim"),
        P("row"),
        P(),
        P(None, "dim", None),
        P(None, "dim"),
    )
    out_specs = (P(None, "dim", None), P(None, "dim", None), P(None, "dim"), P(None, "dim"))
    return jax.shard_map(local, mesh=mesh, in_specs=in_specs, out_specs=out_specs, check_vma=False)
```

```python
import math

import jax
import jax.numpy as jnp
from jax import lax
from jax.experimental import pallas as pl
from jax.experimental.pallas import tpu as pltpu
from jax.sharding import PartitionSpec as P

BLOCK = 128
S = 5
W = 256
R = 64
SUB = 16
XS = S * W // 4
ZS = XS // 4
XP = W // 4
ZP = XP // 4
AHEAD = 6
WINDOW = 4
LAG = 11
MESH = pl.DeviceIdType.MESH
F32 = jnp.float32
BF16 = jnp.bfloat16


def flip(value, mask):
    for bit in (1, 2, 4, 8):
        if mask & bit:
            value = value + bit * (1 - 2 * ((value // bit) % 2))
    return value


def swap(value):
    return jnp.concatenate([value[:, BLOCK:], value[:, :BLOCK]], axis=1)


def fold(value):
    return jnp.sum(value.reshape(-1, 8, value.shape[-1]), axis=0)


def make_kernel(home_rows, total_rows):
    n = home_rows // R
    scale = 1.0 / math.sqrt(total_rows)

    def kernel(
        vec, codes, w, ang, idx, tab, grad_o, ang_o,
        u, v, vp, gs, qs, qp, dv, cod, codsend, wb, trig, ang2, fc, fac, acc, sa, sb,
        sx, rx, sxs, sz, rz, szs, sk, rk, gx,
        lsem, w_s, w_r, t_s, t_r, v_s, v_r, c_s, c_r, f_s, f_r, b_s, b_r, r_s, r_r,
    ):
        d = lax.axis_index("dim")
        r = lax.axis_index("row")
        zh, y, c = d // 8, (d // 2) % 4, d % 2
        x, zl = r // 8, r % 8
        kk, ii = zh * 2 + zl // 4, zl % 4

        def device(zh=zh, y=y, c=c, x=x, kk=None, ii=ii):
            lo = zl // 4
            if kk is not None:
                zh, lo = kk // 2, kk % 2
            return (zh * 8 + y * 2 + c, x * 8 + lo * 4 + ii)

        across = device(zh=1 - zh)
        core = device(c=1 - c)
        y_near, y_far = device(y=flip(y, 1)), device(y=flip(y, 2))
        x_peers = [device(x=flip(x, m)) for m in (1, 2, 3)]
        i_peers = [device(ii=flip(ii, m)) for m in (1, 2, 3)]
        k_peers = [device(kk=flip(kk, m)) for m in (1, 2, 3)]
        partners = [None, core, y_near, y_far]
        greeted = [core, y_near, y_far] + x_peers + i_peers + k_peers

        def remote(src, dst, send, recv, target):
            return pltpu.make_async_remote_copy(
                src_ref=src, dst_ref=dst, send_sem=send, recv_sem=recv,
                device_id=target, device_id_type=MESH,
            )

        barrier = pltpu.get_barrier_semaphore()
        for target in greeted:
            pl.semaphore_signal(barrier, inc=1, device_id=target, device_id_type=MESH)

        wb[0] = w[...].astype(BF16)
        pl.semaphore_wait(barrier, len(greeted))

        home = pl.multiple_of(zh * home_rows, 64)
        away = pl.multiple_of((1 - zh) * home_rows, 64)

        def weight_copy(step):
            whole = pl.ds(pl.multiple_of(x * XS, 64), XS)
            piece = pl.ds(pl.multiple_of(x * XS + ii * ZS, 16), ZS)
            if step == 0:
                source, rows, target = 0, piece, across
            elif step < 4:
                source, rows, target = 1, piece, i_peers[step - 1]
            else:
                source, rows, target = 1, whole, x_peers[step - 4]
            return remote(wb.at[source, rows], wb.at[1, rows], w_s.at[step], w_r.at[step], target)

        def angle_copy():
            return remote(ang, ang2, t_s.at[0], t_r.at[0], across)

        def vec_copy(j):
            rows = pl.ds(pl.multiple_of(away + j * R, 16), R)
            return remote(vec.at[rows], u.at[0, n + j], v_s.at[j], v_r.at[j], across)

        def own_copy(j):
            rows = pl.ds(pl.multiple_of(home + j * R, 16), R)
            return pltpu.make_async_copy(vec.at[rows], u.at[0, j], lsem.at[j])

        def code_copy(j):
            return remote(codsend.at[j], cod.at[j], c_s.at[j], c_r.at[j], across)

        def fwd_copy(s, i):
            return remote(
                v.at[s, i], vp.at[s - 1, i], f_s.at[s - 1, i], f_r.at[s - 1, i], partners[s]
            )

        def bwd_copy(s, j):
            return remote(
                qs.at[s - 1, j], qp.at[s - 1, j], b_s.at[s - 1, j], b_r.at[s - 1, j], partners[s]
            )

        vec_copy(0).start()
        weight_copy(0).start()
        angle_copy().start()
        for j in range(n):
            own_copy(j).start()

        def steps(step, carry=None):
            for k in range(R // SUB):
                carry = step(k, carry)
            return carry

        def rows_of(k):
            return pl.ds(k * SUB, SUB)

        def send_codes(j):
            def step(k, carry):
                rows = pl.ds(pl.multiple_of(away + j * R + k * SUB, 16), SUB)
                codsend[j, rows_of(k)] = codes[rows].astype(F32).astype(BF16)

            steps(step)
            code_copy(j).start()

        for j in range(1, WINDOW):
            vec_copy(j).start()

        lane = lax.broadcasted_iota(jnp.int32, (1, W), 1)
        bits = [jnp.where(lane < BLOCK, 1.0, -1.0).astype(F32)]
        for bit in (c, y % 2, y // 2, zh):
            bits.append(jnp.full((1, W), (1 - 2 * bit).astype(F32), F32))

        def twiddle(h, theta):
            trig[h, 0:S] = jnp.cos(theta)
            sines = jnp.sin(theta)
            for s in range(S):
                sign = bits[s] if (h == 0 or s < 4) else -bits[s]
                trig[h, 8 + s : 9 + s] = sign * sines[s : s + 1]

        twiddle(0, ang[...])
        acc[...] = jnp.zeros_like(acc)
        sa[...] = jnp.zeros_like(sa)
        sb[...] = jnp.zeros_like(sb)
        index = idx[...]
        factor = jnp.zeros(index.shape, F32)
        for level in range(tab.shape[0]):
            factor = jnp.where(index == level, tab[level], factor)
        fc[0 : index.shape[0]] = factor

        def spread(p, carry):
            piece = zh * (home_rows // 64) + p
            row = fc[pl.ds(piece // 2, 1)]
            at = lax.broadcasted_iota(jnp.int32, (64, BLOCK), 1)
            want = lax.broadcasted_iota(jnp.int32, (64, BLOCK), 0) + 64 * (piece % 2)
            column = jnp.sum(jnp.where(at == want, row, 0.0), axis=1, keepdims=True)
            fac[pl.ds(pl.multiple_of(p * 64, 64), 64)] = jnp.broadcast_to(column, (64, BLOCK))
            return carry

        lax.fori_loop(0, home_rows // 64, spread, 0)

        def wrow(s, b):
            return pl.ds(s * W + b * BLOCK, BLOCK)

        def lanes(b):
            return pl.ds(b * BLOCK, BLOCK)

        def cos_of(h, s):
            return trig[h, pl.ds(s, 1)]

        def sin_of(h, s):
            return trig[h, pl.ds(8 + s, 1)]

        def mix(s, i, h):
            for b in range(2):
                v[s, i, :, lanes(b)] = jnp.dot(
                    u[s, i, :, lanes(b)], wb[h, wrow(s, b)], preferred_element_type=F32
                ).astype(BF16)

        def combine(s, i, h):
            cosine, sine = cos_of(h, s), sin_of(h, s)

            def step(k, carry):
                rows = rows_of(k)
                mine = v[s, i, rows].astype(F32)
                theirs = swap(mine) if s == 0 else vp[s - 1, i, rows].astype(F32)
                u[s + 1, i, rows] = (cosine * mine + sine * theirs).astype(BF16)

            steps(step)

        def start(i, h):
            mix(0, i, h)
            combine(0, i, h)
            mix(1, i, h)
            fwd_copy(1, i).start()

        def carry_on(s, i, h):
            fwd_copy(s, i).wait_recv()
            combine(s, i, h)
            mix(s + 1, i, h)
            if s < 3:
                fwd_copy(s + 1, i).start()

        def weight_grad(s, j):
            for h in range(2):
                for b in range(2):
                    acc[h, wrow(s, b)] += lax.dot_general(
                        u[s, h * n + j, :, lanes(b)],
                        dv[h, :, lanes(b)],
                        (((0,), (0,)), ((), ())),
                        preferred_element_type=F32,
                    )

        def pull(s, j):
            t = s - 1
            for h in range(2):
                i = h * n + j
                slot = max(t, 1) - 1
                for b in range(2):
                    gs[slot, j, h, :, lanes(b)] = lax.dot_general(
                        dv[h, :, lanes(b)],
                        wb[h, wrow(s, b)],
                        (((1,), (1,)), ((), ())),
                        preferred_element_type=F32,
                    ).astype(BF16)
            for h in range(2):
                i = h * n + j
                cosine, sine = cos_of(h, t), sin_of(h, t)

                def step(k, sums, h=h, i=i, cosine=cosine, sine=sine):
                    rows = rows_of(k)
                    up = gs[slot, j, h, rows].astype(F32)
                    mine = v[t, i, rows].astype(F32)
                    theirs = swap(mine) if t == 0 else vp[t - 1, i, rows].astype(F32)
                    sent = (sine * up).astype(BF16)
                    if t == 0:
                        dv[h, rows] = (cosine * up + swap(sent.astype(F32))).astype(BF16)
                    else:
                        qs[t - 1, j, h, rows] = sent
                    return sums[0] + fold(up * mine), sums[1] + fold(up * theirs)

                one, two = steps(step, (sa[h, t], sb[h, t]))
                sa[h, t] = one
                sb[h, t] = two

        def turn(j):
            code_copy(j).wait_recv()
            cos_a, sin_a, cos_b, sin_b = cos_of(0, 4), sin_of(0, 4), cos_of(1, 4), sin_of(1, 4)

            def step(k, sums):
                rows = rows_of(k)
                va, vb = v[4, j, rows].astype(F32), v[4, n + j, rows].astype(F32)
                f = fac[pl.ds(pl.multiple_of(j * R + k * SUB, 16), SUB)]
                f = jnp.concatenate([f, f], axis=1)
                own = codes[pl.ds(pl.multiple_of(home + j * R + k * SUB, 16), SUB)].astype(F32)
                recon_a = f * (own - 7.5)
                recon_b = f * (cod[j, rows].astype(F32) - 7.5)
                ua = (cos_a * va + sin_a * vb).astype(BF16).astype(F32)
                ub = (cos_b * vb + sin_b * va).astype(BF16).astype(F32)
                ga = ((ua - recon_a) * scale).astype(BF16).astype(F32)
                gb = ((ub - recon_b) * scale).astype(BF16).astype(F32)
                qa = (sin_a * ga).astype(BF16).astype(F32)
                qb = (sin_b * gb).astype(BF16).astype(F32)
                dv[0, rows] = (cos_a * ga + qb).astype(BF16)
                dv[1, rows] = (cos_b * gb + qa).astype(BF16)
                return (
                    sums[0] + fold(ga * va),
                    sums[1] + fold(ga * vb),
                    sums[2] + fold(gb * vb),
                    sums[3] + fold(gb * va),
                )

            sums = steps(step, (sa[0, 4], sb[0, 4], sa[1, 4], sb[1, 4]))
            sa[0, 4], sb[0, 4], sa[1, 4], sb[1, 4] = sums
            weight_grad(4, j)
            pull(4, j)
            bwd_copy(3, j).start()

        def back(s, j):
            bwd_copy(s, j).wait_recv()
            for h in range(2):
                cosine = cos_of(h, s)

                def step(k, carry, h=h, cosine=cosine):
                    rows = rows_of(k)
                    up = gs[s - 1, j, h, rows].astype(F32)
                    dv[h, rows] = (cosine * up + qp[s - 1, j, h, rows].astype(F32)).astype(BF16)

                steps(step)
            weight_grad(s, j)
            pull(s, j)
            if s > 1:
                bwd_copy(s - 1, j).start()
            else:
                weight_grad(0, j)

        def x_rows(s):
            return pl.ds((S - 1 - s) * 2 * XP, 2 * XP + (32 if s == 0 else 0))

        def x_copy(s, m):
            rows = x_rows(s)
            at = 3 * s + m
            return remote(sx.at[m, rows], rx.at[x, rows], r_s.at[at], r_r.at[at], x_peers[m])

        def x_fill(ref, s, p, angles):
            first = (S - 1 - s) * 2 * XP
            for h in range(2):
                rows = pl.ds(pl.multiple_of(s * W + p * XP, 64), XP)
                ref[pl.ds(first + h * XP, XP)] = acc[h, rows].astype(BF16)
            if s == 0:
                ref[pl.ds(first + 2 * XP, 32)] = angles

        def x_begin(s, angles=None):
            for m in range(3):
                x_fill(sx.at[m], s, flip(x, m + 1), angles)
                x_copy(s, m).start()
            x_fill(rx.at[x], s, x, angles)

        def one_loop(t, carry):
            def at_chunk(offset, last, body):
                j = t - offset

                @pl.when((j >= 0) & (j < n))
                def _():
                    body(j)

                for s in last:

                    @pl.when(j == n - 1)
                    def _(s=s):
                        x_begin(s)

            at_chunk(LAG + 11, (1,), lambda j: back(1, j))
            at_chunk(LAG + 10, (2,), lambda j: back(2, j))
            at_chunk(LAG + 8, (3,), lambda j: back(3, j))
            at_chunk(LAG + 5, (), lambda j: carry_on(3, n + j, 1))
            at_chunk(LAG + 3, (), lambda j: carry_on(2, n + j, 1))
            at_chunk(LAG + 1, (), lambda j: carry_on(1, n + j, 1))
            at_chunk(8, (), lambda j: carry_on(3, j, 0))
            at_chunk(5, (), lambda j: carry_on(2, j, 0))
            at_chunk(2, (), lambda j: carry_on(1, j, 0))

            @pl.when(t == 6)
            def _():
                weight_copy(0).wait_recv()
                for step in (1, 2, 3):
                    weight_copy(step).start()

            @pl.when(t == 8)
            def _():
                for step in (1, 2, 3):
                    weight_copy(step).wait_recv()
                for step in (4, 5, 6):
                    weight_copy(step).start()

            @pl.when(t == LAG)
            def _():
                angle_copy().wait_recv()
                twiddle(1, ang2[...])
                for step in (4, 5, 6):
                    weight_copy(step).wait_recv()

            @pl.when(t < n)
            def _():
                own_copy(t).wait()
                start(t, 0)

            def begin(j):
                vec_copy(j).wait_recv()

                @pl.when(j + WINDOW < n)
                def _():
                    vec_copy(j + WINDOW).start()

                start(n + j, 1)

            at_chunk(LAG, (), begin)
            at_chunk(LAG + 2, (), send_codes)
            at_chunk(LAG + AHEAD, (4,), turn)
            return carry

        lax.fori_loop(0, n + LAG + 11, one_loop, 0)

        turned = []
        for h in range(2):
            parts = []
            for s in range(S):
                a = jnp.sum(sa[h, s], axis=0, keepdims=True)
                b = jnp.sum(sb[h, s], axis=0, keepdims=True)
                sign = bits[s] if (h == 0 or s < 4) else -bits[s]
                whole = sign * (cos_of(h, s) * b - sin_of(h, s) * a)
                parts += [whole[:, :BLOCK], whole[:, BLOCK:]]
            parts.append(jnp.zeros((6, BLOCK), F32))
            turned.append(jnp.concatenate(parts, axis=0).astype(BF16))
        angles = jnp.concatenate(turned, axis=0)

        def z_copy(stage, m):
            at = 3 * (S + stage) + m
            piece = pl.ds(pl.multiple_of(ii * ZS, 16), ZS)
            source, target, peer = (
                (sz.at[m], rz.at[ii], i_peers[m]),
                (sk.at[m], rk.at[kk], k_peers[m]),
                (gx.at[x, piece], gx.at[x, piece], i_peers[m]),
                (gx.at[x], gx.at[x], x_peers[m]),
            )[stage]
            return remote(source, target, r_s.at[at], r_r.at[at], peer)

        def total(ref):
            return (ref[0].astype(F32) + ref[1].astype(F32)) + (
                ref[2].astype(F32) + ref[3].astype(F32)
            )

        def z_fill(ref, p):
            for h in range(2):
                for s in range(S):
                    first = (S - 1 - s) * 2 * XP + h * XP
                    rows = pl.ds(pl.multiple_of(first + p * ZP, 16), ZP)
                    ref[pl.ds((h * S + s) * ZP, ZP)] = sxs[rows].astype(BF16)
            ref[pl.ds(2 * ZS, 32)] = sxs[pl.ds(2 * XS, 32)].astype(BF16)

        def k_fill(ref, h):
            ref[pl.ds(0, ZS)] = szs[pl.ds(h * ZS, ZS)].astype(BF16)
            ref[pl.ds(ZS, 16)] = szs[pl.ds(2 * ZS + h * 16, 16)].astype(BF16)

        x_begin(0, angles)
        for s in reversed(range(S)):
            for m in range(3):
                x_copy(s, m).wait_recv()
        sxs[...] = total(rx)
        for m in range(3):
            z_fill(sz.at[m], flip(ii, m + 1))
            z_copy(0, m).start()
        z_fill(rz.at[ii], ii)
        for m in range(3):
            z_copy(0, m).wait_recv()
        szs[...] = total(rz)
        for m in range(3):
            k_fill(sk.at[m], 0 if m == 0 else 1)
            z_copy(1, m).start()
        k_fill(rk.at[kk], 0)
        for m in range(3):
            z_copy(1, m).wait_recv()
        final = total(rk)
        gx[x, pl.ds(pl.multiple_of(ii * ZS, 16), ZS)] = final[:ZS].astype(BF16)
        for m in range(3):
            z_copy(2, m).start()
        ang_o[...] = final[ZS:]
        for m in range(3):
            z_copy(2, m).wait_recv()
        for m in range(3):
            z_copy(3, m).start()
        for m in range(3):
            z_copy(3, m).wait_recv()
        for p in range(4):
            for q in range(4):
                for s in range(S):
                    grad_o[pl.ds(s * W + p * XP + q * ZP, ZP)] = gx[
                        p, pl.ds(q * ZS + s * ZP, ZP)
                    ].astype(F32)

        for step in range(7):
            weight_copy(step).wait_send()
        angle_copy().wait_send()

        def drain(j, carry):
            vec_copy(j).wait_send()
            code_copy(j).wait_send()
            for s in (1, 2, 3):
                fwd_copy(s, j).wait_send()
                fwd_copy(s, n + j).wait_send()
                bwd_copy(s, j).wait_send()
            return carry

        lax.fori_loop(0, n, drain, 0)
        for m in range(3):
            for s in range(S):
                x_copy(s, m).wait_send()
            for stage in range(4):
                z_copy(stage, m).wait_send()

    return kernel, n


def gradients(vectors, blocks, angles, codes, scale_index, scale_table):
    num_rows = vectors.shape[0]
    kernel, n = make_kernel(num_rows // 2, num_rows * 32)
    vmem = pl.BlockSpec(memory_space=pltpu.VMEM)
    dma = pltpu.SemaphoreType.DMA
    shapes = [
        pltpu.VMEM((S, 2 * n, R, W), BF16),
        pltpu.VMEM((S, 2 * n, R, W), BF16),
        pltpu.VMEM((3, 2 * n, R, W), BF16),
        pltpu.VMEM((3, n, 2, R, W), BF16),
        pltpu.VMEM((3, n, 2, R, W), BF16),
        pltpu.VMEM((3, n, 2, R, W), BF16),
        pltpu.VMEM((2, R, W), BF16),
        pltpu.VMEM((n, R, W), BF16),
        pltpu.VMEM((n, R, W), BF16),
        pltpu.VMEM((2, S * W, BLOCK), BF16),
        pltpu.VMEM((2, 16, W), F32),
        pltpu.VMEM((S, W), F32),
        pltpu.VMEM((16, BLOCK), F32),
        pltpu.VMEM((num_rows // 2, BLOCK), F32),
        pltpu.VMEM((2, S * W, BLOCK), F32),
        pltpu.VMEM((2, S, 8, W), F32),
        pltpu.VMEM((2, S, 8, W), F32),
        pltpu.VMEM((3, 2 * XS + 32, BLOCK), BF16),
        pltpu.VMEM((4, 2 * XS + 32, BLOCK), BF16),
        pltpu.VMEM((2 * XS + 32, BLOCK), F32),
        pltpu.VMEM((3, 2 * ZS + 32, BLOCK), BF16),
        pltpu.VMEM((4, 2 * ZS + 32, BLOCK), BF16),
        pltpu.VMEM((2 * ZS + 32, BLOCK), F32),
        pltpu.VMEM((3, ZS + 16, BLOCK), BF16),
        pltpu.VMEM((4, ZS + 16, BLOCK), BF16),
        pltpu.VMEM((4, XS, BLOCK), BF16),
        dma((n,)),
        dma((7,)), dma((7,)), dma((1,)), dma((1,)), dma((n,)), dma((n,)), dma((n,)), dma((n,)),
        dma((3, 2 * n)), dma((3, 2 * n)), dma((3, n)), dma((3, n)),
        dma((27,)), dma((27,)),
    ]
    return pl.pallas_call(
        kernel,
        name="butterfly",
        out_shape=(
            jax.ShapeDtypeStruct((S * W, BLOCK), F32),
            jax.ShapeDtypeStruct((16, BLOCK), F32),
        ),
        in_specs=[
            pl.BlockSpec(memory_space=pl.ANY),
            vmem, vmem, vmem, vmem,
            pl.BlockSpec(memory_space=pltpu.SMEM),
        ],
        out_specs=(vmem, vmem),
        scratch_shapes=shapes,
        compiler_params=pltpu.CompilerParams(
            collective_id=0, has_side_effects=True, vmem_limit_bytes=56 * 2**20
        ),
    )(
        vectors, codes, blocks.reshape(S * W, BLOCK), angles,
        scale_index.reshape(num_rows // BLOCK, BLOCK), scale_table,
    )


def local(vectors, blocks, angles, codes, scale_index, scale_table, block_state, angle_state):
    grad, turned = gradients(vectors, blocks, angles, codes, scale_index, scale_table)
    grad_blocks = grad.reshape(S, W, BLOCK)
    grad_angles = turned[: 2 * S].reshape(S, W)
    new_block_state = 0.9 * block_state + 0.1 * grad_blocks * grad_blocks
    step_blocks = grad_blocks / jnp.sqrt(new_block_state)
    new_angle_state = 0.9 * angle_state + 0.1 * grad_angles * grad_angles
    step_angles = grad_angles / jnp.sqrt(new_angle_state)
    return (step_blocks, new_block_state, step_angles, new_angle_state)


def solution(mesh):
    in_specs = (
        P("row", "dim"),
        P(None, "dim", None),
        P(None, "dim"),
        P("row", "dim"),
        P("row"),
        P(),
        P(None, "dim", None),
        P(None, "dim"),
    )
    out_specs = (P(None, "dim", None), P(None, "dim", None), P(None, "dim"), P(None, "dim"))
    return jax.shard_map(local, mesh=mesh, in_specs=in_specs, out_specs=out_specs, check_vma=False)
```
